32 devices in a mesh: grp: 4 (over y, x), dev: 8 (over z, core).
Axes of the slice: x: 2, y: 2, z: 4, core: 2. Of those that a mesh axis runs over, the one named last changes fastest.
Arguments:
- queries: bfloat16 [4096, 256], P(('grp', 'dev')), may hold values from -32 to 32
- items: bfloat16 [4096, 256], P(('grp', 'dev')), may hold values from -24 to 24
- item_ids: int32 [4096], P('grp'), may hold values from 0 to 262143
- neg_embed: bfloat16 [4096, 256], P('dev'), may hold values from -6 to 6
- neg_logq: float32 [4096], P('dev'), may hold values from -12 to -8
- logq_table: float32 [262144], replicated, may hold values from -11 to -9.5
Outputs:
- query_loss: float32 [4096], P(('grp', 'dev'))
- query_grad: float32 [4096, 256], P(('grp', 'dev'))
- item_grad: float32 [4096, 256], P(('grp', 'dev'))
- negative_grad: float32 [4096, 256], P('dev')
The draws below stay inside these ranges and needn't reach their ends.
Inputs may be any that keep to these rules, and one draw needn't show every extreme that they name: `item_ids`: a row of logq_table.
All inputs are finite; a program needn't handle non-finite values.
Results may differ from the reference program's by a relative error of at most 0.0036.
Values may be sent and summed in bfloat16 or wider, within the bound.
No kernel may reach another device: no remote copies, remote signals or barrier semaphores. Data moves between devices by JAX's collectives and lax.ppermute only.
A program may use at most 64 MiB of HBM per device.

```python
import math
import jax
import jax.numpy as jnp
import numpy as np
from jax import lax

D = 256
VOCAB = 262144
GROUP_ROWS = 1024
BATCH = 4096
NEG = 4096
N_GRP = 4


def joint_pair(key):
    base = jax.random.fold_in(key, 11)
    keys = jax.random.split(base, 8)
    queries = jax.random.normal(keys[0], (BATCH, D), jnp.float32)
    items = jax.random.normal(keys[1], (BATCH, D), jnp.float32)
    positions = jnp.arange(BATCH)
    leading = positions % 32 == 5
    trailing = positions % 32 == 6
    strength = jax.random.uniform(keys[4], (BATCH, 1), jnp.float32, 1.5, 2.5)
    target = jax.random.uniform(keys[7], (BATCH, 1), jnp.float32, 110.0, 320.0)
    squared = jnp.sum(items * items, axis=1, keepdims=True)
    lifted = items * jnp.sqrt(target / (0.25 * strength * squared))
    items = jnp.where(leading[:, None], lifted, items)
    spacing = jax.random.uniform(keys[5], (BATCH, 1), jnp.float32, 2.0, 2.5)
    lead_squared = jnp.sum(items * items, axis=1, keepdims=True)
    shrink = spacing / (0.25 * strength * lead_squared)
    follower = jnp.roll(items * (1.0 - shrink), 1, axis=0) + 0.005 * jax.random.normal(keys[6], (BATCH, D), jnp.float32)
    items = jnp.where(trailing[:, None], follower, items)
    queries = jnp.where(leading[:, None], strength * items, queries)
    return (jnp.clip(queries, -32.0, 32.0), jnp.clip(items, -24.0, 24.0))


def draw_queries(key, part):
    return joint_pair(key)[0].astype(jnp.bfloat16)


def draw_items(key, part):
    return joint_pair(key)[1].astype(jnp.bfloat16)


def touch_ends(entries, key, smallest, high):
    extent = entries.shape
    index_at = [jax.random.randint(jax.random.fold_in(key, axis), (), 0, extent[axis]) for axis in range(len(extent))]
    entries = entries.at[tuple(index_at)].set(smallest)
    longest = extent.index(max(extent))
    index_at[longest] = (index_at[longest] + 1) % extent[longest]
    return entries.at[tuple(index_at)].set(high)


def level_of(rng, extent, cuts, smallest, top_value):
    loudness, own = 1.0, jax.random.fold_in(rng, 6)
    for position, parts in cuts:
        steps = jnp.exp(jax.random.uniform(jax.random.fold_in(own, position), (parts,), jnp.float32, smallest / len(cuts), top_value / len(cuts)))
        loudness = loudness * jnp.repeat(steps, extent[position] // parts).reshape([-1 if axis == position else 1 for axis in range(len(extent))])
    return loudness


def ranked_wide(own_key, dims, count, lean):
    portions = [min(1 << octave, count + 1 - (1 << octave)) * (1 << 20) // math.isqrt((1 << octave) ** lean) + 1 for octave in range((count + 1).bit_length()) if 1 << octave <= count]
    scale = 1 + sum(portions) // (1 << 30)
    grid = np.cumsum(np.array([max(1, weight // scale) for weight in portions]))
    lot = jax.random.randint(jax.random.fold_in(own_key, 1), dims, 0, int(grid[len(portions) - 1]))
    start = jnp.left_shift(1, jnp.searchsorted(jnp.asarray(grid, jnp.int32), lot, side="right").astype(jnp.int32))
    grade = start - 1 + jax.random.randint(jax.random.fold_in(own_key, 4), dims, 0, 1 << 30) % jnp.minimum(start, count + 1 - start)
    return jax.random.permutation(jax.random.fold_in(own_key, 2), count)[grade].astype(jnp.int32)


def centred(own_key, extent, deviation, bound, pieces=(), kind=jnp.bfloat16):
    gain = level_of(own_key, extent, pieces, -0.22, 0.18) if pieces else 1.0
    result = jax.random.normal(own_key, extent, jnp.float32) * deviation * gain
    return jnp.minimum(jnp.maximum(result, -bound), bound).astype(kind)


def setup_inputs(seed: int = 0) -> dict:
    arg_keys = jax.random.split(jax.random.key(seed), 7)
    queries = draw_queries(jax.random.fold_in(arg_keys[6], 71), 0)
    items = draw_items(jax.random.fold_in(arg_keys[6], 71), 0)
    item_ids = touch_ends(ranked_wide(arg_keys[2], (BATCH,), VOCAB, 2), jax.random.fold_in(arg_keys[2], 3), 0, VOCAB - 1).astype(jnp.int32)
    neg_embed = centred(arg_keys[3], (NEG, D), 1.0, 6.0, ((0, 8),))
    neg_logq = jnp.clip(-12.0 + 4.0 * jax.random.uniform(arg_keys[4], (NEG,), jnp.float32) ** level_of(arg_keys[4], (NEG,), ((0, 8),), -0.2, 0.2), -12.0, -8.0)
    logq_table = jnp.clip(jax.random.uniform(arg_keys[5], (VOCAB,), jnp.float32, -11.0, -9.5), -11.0, -9.5)
    return {"queries": queries, "items": items, "item_ids": item_ids, "neg_embed": neg_embed, "neg_logq": neg_logq, "logq_table": logq_table}


logit_scale = 0.25


def reference(queries, items, item_ids, neg_embed, neg_logq, logq_table):
    item_offsets = jnp.take(logq_table, item_ids, axis=0)
    block_rows = min(512, GROUP_ROWS)
    block_count = GROUP_ROWS // block_rows
    grouped_q = queries.reshape(N_GRP, GROUP_ROWS, D)
    grouped_v = items.reshape(N_GRP, GROUP_ROWS, D)
    grouped_off = item_offsets.reshape(N_GRP, GROUP_ROWS)

    def one_group(packed):
        group_q, group_v, group_off = packed
        candidates = jnp.concatenate([group_v, neg_embed], axis=0)
        cand_offsets = jnp.concatenate([group_off, neg_logq], axis=0)
        columns = jnp.arange(GROUP_ROWS + NEG, dtype=jnp.int32)

        def one_block(summed, block_idx):
            first_row = block_idx * block_rows
            q_block = lax.dynamic_slice_in_dim(group_q, first_row, block_rows, 0)
            scores = logit_scale * jnp.dot(q_block, candidates.T, preferred_element_type=jnp.float32) - cand_offsets[None, :]
            row_max = jnp.max(scores, axis=1)
            log_norm = row_max + jnp.log(jnp.sum(jnp.exp(scores - row_max[:, None]), axis=1))
            targets = first_row + jnp.arange(block_rows, dtype=jnp.int32)
            positive_mask = columns[None, :] == targets[:, None]
            matched = jnp.sum(jnp.where(positive_mask, scores, 0.0), axis=1)
            logit_grad = (logit_scale * (jnp.exp(scores - log_norm[:, None]) - positive_mask.astype(jnp.float32))).astype(jnp.bfloat16)
            summed = summed + jnp.dot(logit_grad.T, q_block, preferred_element_type=jnp.float32)
            return summed, (log_norm - matched, jnp.dot(logit_grad, candidates, preferred_element_type=jnp.float32))

        zero_acc = jnp.zeros((GROUP_ROWS + NEG, D), jnp.float32)
        cand_grad, (losses, q_grads) = lax.scan(one_block, zero_acc, jnp.arange(block_count, dtype=jnp.int32))
        return losses.reshape(GROUP_ROWS), q_grads.reshape(GROUP_ROWS, D), cand_grad[:GROUP_ROWS], cand_grad[GROUP_ROWS:]

    losses, q_grads, v_grads, n_grads = lax.map(one_group, (grouped_q, grouped_v, grouped_off))
    return (losses.reshape(BATCH), q_grads.reshape(BATCH, D), v_grads.reshape(BATCH, D), jnp.sum(n_grads, axis=0))
```

```python
import jax
import jax.numpy as jnp
from jax import lax
from jax.experimental import pallas as pl
from jax.experimental.pallas import tpu as pltpu
from jax.sharding import PartitionSpec as P

logit_scale = 0.25
VMEM = pl.BlockSpec(memory_space=pltpu.VMEM)
F32, BF16 = jnp.float32, jnp.bfloat16
NT = (((1,), (1,)), ((), ()))


def round_up(x, m):
    return -(-x // m) * m


def swap(x, axis, count, mask):
    return lax.ppermute(x, axis, [(i, i ^ mask) for i in range(count)])


def fold(x, op):
    rows, cols = x.shape
    return op(x.reshape(rows // 8, 8, cols), axis=0)


def pad_rows(parts, multiple):
    have = sum(p.shape[0] for p in parts)
    lack = round_up(have, multiple) - have
    if lack:
        parts = parts + [jnp.zeros((lack, parts[0].shape[1]), parts[0].dtype)]
    return jnp.concatenate(parts, axis=0)


def offset_columns(rows, pieces):
    flipped = pad_rows(rows, 8).T
    return [flipped[:, j : j + 1] for j in range(pieces)]


def split3(x):
    hi = x.astype(BF16)
    rest = x - hi.astype(F32)
    mid = rest.astype(BF16)
    return (hi, mid, (rest - mid.astype(F32)).astype(BF16))


def candidate_rows(refs, offs, rows):
    out = []
    for ref, off in zip(refs, offs):
        for j in range(ref.shape[0] // rows):
            out.append((ref, j * rows, off[j : j + 1, :]))
    return out


def forward_kernel(n, *refs):
    q_refs, refs = refs[:n], refs[n:]
    c_refs, refs = refs[:4], refs[4:]
    off_refs, refs = refs[:4], refs[4:]
    own_ref, lse_ref, msg_refs = refs[0], refs[1], refs[2 : 2 + n - 1]
    q_all, c_t, s_all, e_all = refs[2 + n - 1 :]
    rows, width = q_refs[0].shape
    runs = candidate_rows(c_refs, [r[...] for r in off_refs], rows)
    cols = offset_columns([r[2] for r in runs], len(runs))
    for k in range(n):
        q_all[k * rows : (k + 1) * rows, :] = q_refs[k][...]
    for j, (ref, first, _) in enumerate(runs):
        c_t[:, j * rows : (j + 1) * rows] = ref[first : first + rows, :].T
    per = 2 if n % 2 == 0 else 1
    chunk = per * rows
    for p in range(n // per):
        q = q_all[p * chunk : (p + 1) * chunk, :]
        top = None
        for j, (ref, first, _) in enumerate(runs):
            s = lax.dot_general(ref[first : first + rows, :], q, NT, preferred_element_type=F32)
            s = logit_scale * s - cols[j]
            s_all[j * rows : (j + 1) * rows, :] = s
            here = fold(s, jnp.max)
            top = here if top is None else jnp.maximum(top, here)
        row_max = jnp.max(top, axis=0, keepdims=True)
        total = None
        for j in range(len(runs)):
            e = jnp.exp(s_all[j * rows : (j + 1) * rows, :] - row_max)
            e_all[j * rows : (j + 1) * rows, :] = e.astype(BF16)
            here = fold(e, jnp.sum)
            total = here if total is None else total + here
        row_sum = jnp.sum(total, axis=0, keepdims=True)
        lse = row_max + jnp.log(row_sum)
        u = jnp.dot(c_t[...], e_all[...], preferred_element_type=F32) / row_sum
        for i in range(per):
            k = p * per + i
            lse_ref[k : k + 1, :] = lse[:, i * rows : (i + 1) * rows]
            u_k = u[:, i * rows : (i + 1) * rows]
            if k == 0:
                own_ref[...] = u_k
            else:
                msg_refs[k - 1][:width, :] = u_k.astype(BF16)
    parts = split3(lse_ref[...])
    block = pad_rows(list(parts), 16)
    for k in range(1, n):
        msg_refs[k - 1][width:, :] = block


def merged_lse(n, lse_ref, msg_refs, width):
    mine = lse_ref[...]
    all_lse = [mine]
    for k in range(1, n):
        got = msg_refs[k - 1][width:, :].astype(F32)
        all_lse.append(got[:n] + got[n : 2 * n] + got[2 * n : 3 * n])
    norms = []
    for b in range(n):
        rows = [all_lse[k][k ^ b : (k ^ b) + 1, :] for k in range(n)]
        top = rows[0]
        for r in rows[1:]:
            top = jnp.maximum(top, r)
        total = jnp.exp(rows[0] - top)
        for r in rows[1:]:
            total = total + jnp.exp(r - top)
        norms.append(top + jnp.log(total))
    return all_lse, norms


def gradient(n, q_all, runs, cols, norms, mask_first, e_all, emit):
    rows = q_all.shape[0] // n
    per = 2 if n % 2 == 0 else 1
    chunk = per * rows
    matched = None
    for j, (ref, first, _) in enumerate(runs):
        cand = ref[first : first + rows, :]
        for p in range(n // per):
            norm = jnp.concatenate(norms[p * per : (p + 1) * per], axis=1)
            q = q_all[p * chunk : (p + 1) * chunk, :]
            s = lax.dot_general(cand, q, NT, preferred_element_type=F32)
            s = logit_scale * s - cols[j]
            prob = jnp.exp(s - norm)
            if mask_first and j == 0 and p == 0:
                r = lax.broadcasted_iota(jnp.int32, s.shape, 0)
                c = lax.broadcasted_iota(jnp.int32, s.shape, 1)
                hit = r == c
                matched = jnp.sum(jnp.where(hit, s, 0.0), axis=0, keepdims=True)[:, :rows]
                prob = prob - hit.astype(F32)
            e_all[:, p * chunk : (p + 1) * chunk] = (logit_scale * prob).astype(BF16)
        emit(j, jnp.dot(e_all[...], q_all[...], preferred_element_type=F32))
    return matched


def partner_kernel(n, *refs):
    q_refs, refs = refs[:n], refs[n:]
    c_refs, refs = refs[:2], refs[2:]
    off_refs, refs = refs[:2], refs[2:]
    lse_ref, refs = refs[0], refs[1:]
    msg_refs, refs = refs[: n - 1], refs[n - 1 :]
    out_ref, q_all, e_all = refs
    rows, width = q_refs[0].shape
    for k in range(n):
        q_all[k * rows : (k + 1) * rows, :] = q_refs[k][...]
    runs = candidate_rows(c_refs, [r[...] for r in off_refs], rows)
    cols = offset_columns([r[2] for r in runs], len(runs))
    _, norms = merged_lse(n, lse_ref, msg_refs, width)

    def emit(j, g):
        out_ref[j * rows : (j + 1) * rows, :] = g.astype(BF16)

    gradient(n, q_all, runs, cols, norms, False, e_all, emit)


def own_kernel(n, *refs):
    q_refs, refs = refs[:n], refs[n:]
    c_refs, refs = refs[:2], refs[2:]
    off_refs, refs = refs[:2], refs[2:]
    lse_ref, own_ref, refs = refs[0], refs[1], refs[2:]
    msg_refs, refs = refs[: n - 1], refs[n - 1 :]
    loss_ref, qg_ref, item_ref, neg_ref, q_all, e_all = refs
    rows, width = q_refs[0].shape
    for k in range(n):
        q_all[k * rows : (k + 1) * rows, :] = q_refs[k][...]
    runs = candidate_rows(c_refs, [r[...] for r in off_refs], rows)
    cols = offset_columns([r[2] for r in runs], len(runs))
    all_lse, norms = merged_lse(n, lse_ref, msg_refs, width)

    def emit(j, g):
        if j == 0:
            item_ref[...] = g
        else:
            neg_ref[(j - 1) * rows : j * rows, :] = g

    matched = gradient(n, q_all, runs, cols, norms, True, e_all, emit)
    loss_ref[...] = norms[0] - matched
    total = jnp.exp(all_lse[0][0:1, :] - norms[0]) * own_ref[...]
    for k in range(1, n):
        weight = jnp.exp(all_lse[k][k : k + 1, :] - norms[0])
        total = total + weight * msg_refs[k - 1][:width, :].astype(F32)
    qg_ref[...] = logit_scale * (total.T - c_refs[0][...].astype(F32))


def local_fn(mesh):
    n_dev, n_grp = mesh.shape["dev"], mesh.shape["grp"]
    n = n_dev // 2

    def local(queries, items, item_ids, neg_embed, neg_logq, logq_table):
        rows, width = queries.shape
        negs = neg_embed.shape[0]
        dev = lax.axis_index("dev")
        q = [queries] + [swap(queries, "dev", n_dev, 2 * k) for k in range(1, n)]
        items_p = swap(items, "dev", n_dev, 1)
        neg_p = swap(neg_embed, "dev", n_dev, 1)
        logq_p = swap(neg_logq, "dev", n_dev, 1)
        pair_ids = lax.dynamic_slice_in_dim(item_ids, (dev // 2) * (2 * rows), 2 * rows, 0)
        pair_off = logq_table.at[pair_ids].get(mode="promise_in_bounds").reshape(2, rows)
        core = dev % 2
        off_o = lax.dynamic_slice_in_dim(pair_off, core, 1, 0)
        off_p = lax.dynamic_slice_in_dim(pair_off, 1 - core, 1, 0)
        lq_o = neg_logq.reshape(negs // rows, rows)
        lq_p = logq_p.reshape(negs // rows, rows)

        cands = 2 * (rows + negs)
        chunk = (2 if n % 2 == 0 else 1) * rows
        msg_rows = width + round_up(3 * n, 16)
        shape = jax.ShapeDtypeStruct
        pairs = cands * n * rows

        own_u, lse, *msgs = pl.pallas_call(
            lambda *r: forward_kernel(n, *r),
            name="fwd",
            out_shape=[shape((width, rows), F32), shape((n, rows), F32)]
            + [shape((msg_rows, rows), BF16)] * (n - 1),
            in_specs=[VMEM] * (n + 8),
            out_specs=[VMEM] * (n + 1),
            scratch_shapes=[
                pltpu.VMEM((n * rows, width), BF16),
                pltpu.VMEM((width, cands), BF16),
                pltpu.VMEM((cands, chunk), F32),
                pltpu.VMEM((cands, chunk), BF16),
            ],
            cost_estimate=pl.CostEstimate(
                flops=4 * pairs * width, bytes_accessed=4 * cands * width, transcendentals=pairs
            ),
        )(*q, items, items_p, neg_embed, neg_p, off_o, off_p, lq_o, lq_p)

        got = [swap(msgs[k - 1], "dev", n_dev, 2 * k) for k in range(1, n)]

        half_cost = pl.CostEstimate(
            flops=2 * pairs * width, bytes_accessed=4 * cands * width, transcendentals=pairs // 2
        )
        half_scratch = [
            pltpu.VMEM((n * rows, width), BF16),
            pltpu.VMEM((rows, n * rows), BF16),
        ]
        theirs = pl.pallas_call(
            lambda *r: partner_kernel(n, *r),
            name="partner",
            out_shape=shape((rows + negs, width), BF16),
            in_specs=[VMEM] * (2 * n + 4),
            out_specs=VMEM,
            scratch_shapes=half_scratch,
            cost_estimate=half_cost,
        )(*q, items_p, neg_p, off_p, lq_p, lse, *got)
        back = swap(theirs, "dev", n_dev, 1)
        loss, query_grad, item_part, neg_part = pl.pallas_call(
            lambda *r: own_kernel(n, *r),
            name="own",
            out_shape=[
                shape((1, rows), F32),
                shape((rows, width), F32),
                shape((rows, width), F32),
                shape((negs, width), F32),
            ],
            in_specs=[VMEM] * (2 * n + 5),
            out_specs=[VMEM] * 4,
            scratch_shapes=half_scratch,
            cost_estimate=half_cost,
        )(*q, items, neg_embed, off_o, lq_o, lse, own_u, *got)

        item_grad = item_part + back[:rows].astype(F32)
        total = neg_part + back[rows:].astype(F32)
        masks = [1 << i for i in range((n_grp - 1).bit_length())]
        steps = len(masks)
        share = negs // steps if steps and negs % (16 * steps) == 0 else negs
        parts = []
        for i in range(negs // share):
            part = total[i * share : (i + 1) * share]
            for t in range(steps):
                part = part.astype(BF16)
                other = swap(part, "grp", n_grp, masks[(i + t) % steps])
                part = part.astype(F32) + other.astype(F32)
            parts.append(part)
        negative_grad = jnp.concatenate(parts, axis=0) if len(parts) > 1 else parts[0]
        return (loss.reshape(rows), query_grad, item_grad, negative_grad)

    return local


def solution(mesh):
    return jax.shard_map(
        local_fn(mesh),
        mesh=mesh,
        in_specs=(
            P(("grp", "dev"), None),
            P(("grp", "dev"), None),
            P("grp"),
            P("dev", None),
            P("dev"),
            P(),
        ),
        out_specs=(
            P(("grp", "dev")),
            P(("grp", "dev"), None),
            P(("grp", "dev"), None),
            P("dev", None),
        ),
        check_vma=False,
    )
```

```python
import jax
import jax.numpy as jnp
from jax import lax
from jax.experimental import pallas as pl
from jax.experimental.pallas import tpu as pltpu
from jax.sharding import PartitionSpec as P

logit_scale = 0.25
LANES = 128
F32, BF16 = jnp.float32, jnp.bfloat16
NT = (((1,), (1,)), ((), ()))
GRANT = 16 << 20


def round_up(x, m):
    return -(-x // m) * m


def swap(x, axis, count, mask):
    return lax.ppermute(x, axis, [(i, i ^ mask) for i in range(count)])


def fold(x, op):
    rows, cols = x.shape
    return op(x.reshape(rows // 8, 8, cols), axis=0)


def pad_rows(parts, multiple):
    have = sum(p.shape[0] for p in parts)
    lack = round_up(have, multiple) - have
    if lack:
        parts = parts + [jnp.zeros((lack, parts[0].shape[1]), parts[0].dtype)]
    return jnp.concatenate(parts, axis=0)


def split3(x):
    hi = x.astype(BF16)
    rest = x - hi.astype(F32)
    mid = rest.astype(BF16)
    return [hi, mid, (rest - mid.astype(F32)).astype(BF16)]


def runs_of(refs, rows):
    return [(ref, first) for ref in refs for first in range(0, ref.shape[0], rows)]


def scores(ref, first, rows, q, col):
    s = lax.dot_general(ref[first : first + rows, :], q, NT, preferred_element_type=F32)
    return logit_scale * s - col


def log_total(runs, cols_ref, q, s_all):
    rows = q.shape[0]
    top = None
    for j, (ref, first) in enumerate(runs):
        s = scores(ref, first, rows, q, cols_ref[:, j : j + 1])
        s_all[j * rows : (j + 1) * rows, :] = s
        here = fold(s, jnp.max)
        top = here if top is None else jnp.maximum(top, here)
    row_max = jnp.max(top, axis=0, keepdims=True)
    total = None
    for j in range(len(runs)):
        here = fold(jnp.exp(s_all[j * rows : (j + 1) * rows, :] - row_max), jnp.sum)
        total = here if total is None else total + here
    return row_max + jnp.log(jnp.sum(total, axis=0, keepdims=True))


def own_block_kernel(ids_ref, table_ref, q_ref, *refs):
    (it_o, neg_o, lq_o, it_p, neg_p, lq_p), refs = refs[:6], refs[6:]
    lse_ref, cols_ref, ct_ref, q_copy, it_copy, neg_copy, picked, s_all = refs
    c_refs = (it_o, it_p, neg_o, neg_p)
    rows, _ = q_ref.shape
    q_copy[...] = q_ref[...]
    it_copy[...] = it_o[...]
    neg_copy[...] = neg_o[...]
    dev = lax.axis_index("dev")
    lane = lax.broadcasted_iota(jnp.int32, (1, LANES), 1)
    for half, owner in enumerate((dev, dev ^ 1)):
        start = owner * rows

        def pick(i, carry, half=half, start=start):
            for t in range(8):
                j = i * 8 + t
                item = ids_ref[start + j]
                row = table_ref[pl.ds(lax.shift_right_logical(item, 7), 1), :]
                picked[pl.ds(half * rows + j, 1), :] = jnp.where(lane == (item & (LANES - 1)), row, 0.0)
            return carry

        lax.fori_loop(0, rows // 8, pick, 0)
    for half in range(2):
        part = picked[half * rows : (half + 1) * rows, :]
        cols_ref[:, half : half + 1] = jnp.sum(part, axis=1, keepdims=True)
    lq = pad_rows([lq_o[...], lq_p[...]], 8).T
    count = lq_o.shape[0] + lq_p.shape[0]
    cols_ref[:, 2 : 2 + count] = lq[:, :count]
    runs = runs_of(c_refs, rows)
    for j, (ref, first) in enumerate(runs):
        ct_ref[:, j * rows : (j + 1) * rows] = ref[first : first + rows, :].T
    lse_ref[...] = log_total(runs, cols_ref, q_ref[...], s_all)


def other_blocks_kernel(n, *refs):
    q_refs, refs = refs[: n - 1], refs[n - 1 :]
    c_refs, (cols_ref, lse0_ref), (lse_ref, msg_ref, s_all) = refs[:4], refs[4:6], refs[6:]
    rows, _ = q_refs[0].shape
    runs = runs_of(c_refs, rows)
    lse_ref[0:1, :] = lse0_ref[...]
    for k in range(1, n):
        lse_ref[k : k + 1, :] = log_total(runs, cols_ref, q_refs[k - 1][...], s_all)
    msg_ref[...] = pad_rows(split3(lse_ref[...]), 16)


def gradient(n, q_all, runs, cols, norm_ref, mask_first, p_ref, emit):
    rows = q_all.shape[0] // n
    per = 2 if n % 2 == 0 else 1
    chunk = per * rows
    matched = None
    for j, (ref, first) in enumerate(runs):
        for p in range(n // per):
            norm = jnp.concatenate([norm_ref[b : b + 1, :] for b in range(p * per, (p + 1) * per)], axis=1)
            q = q_all[p * chunk : (p + 1) * chunk, :]
            s = scores(ref, first, rows, q, cols[j]) if per == 1 else (
                logit_scale
                * lax.dot_general(ref[first : first + rows, :], q, NT, preferred_element_type=F32)
                - cols[j]
            )
            prob = jnp.exp(s - norm)
            if mask_first and j == 0 and p == 0:
                hit = lax.broadcasted_iota(jnp.int32, s.shape, 0) == lax.broadcasted_iota(
                    jnp.int32, s.shape, 1
                )
                matched = jnp.sum(jnp.where(hit, s, 0.0), axis=0, keepdims=True)[:, :rows]
                prob = prob - hit.astype(F32)
            p_ref[j * rows : (j + 1) * rows, p * chunk : (p + 1) * chunk] = (logit_scale * prob).astype(BF16)
        emit(j, jnp.dot(p_ref[j * rows : (j + 1) * rows, :], q_all[...], preferred_element_type=F32))
    return matched


def partner_kernel(n, first_col, *refs):
    q_refs, refs = refs[:n], refs[n:]
    neg_ref, cols_ref, lse_ref, refs = refs[0], refs[1], refs[2], refs[3:]
    got_refs, (out_ref, p_ref, norm_ref, q_all) = refs[: n - 1], refs[n - 1 :]
    rows, _ = q_refs[0].shape
    for k in range(n):
        q_all[k * rows : (k + 1) * rows, :] = q_refs[k][...]
    totals = [lse_ref[...]]
    for ref in got_refs:
        got = ref[...].astype(F32)
        totals.append(got[:n] + got[n : 2 * n] + got[2 * n : 3 * n])
    for b in range(n):
        parts = [totals[k][k ^ b : (k ^ b) + 1, :] for k in range(n)]
        top = parts[0]
        for r in parts[1:]:
            top = jnp.maximum(top, r)
        total = jnp.exp(parts[0] - top)
        for r in parts[1:]:
            total = total + jnp.exp(r - top)
        norm_ref[b : b + 1, :] = top + jnp.log(total)
    runs = runs_of([neg_ref], rows)
    cols = [cols_ref[:, first_col + j : first_col + j + 1] for j in range(len(runs))]

    def emit(j, g):
        out_ref[j * rows : (j + 1) * rows, :] = g.astype(BF16)

    gradient(n, q_all, runs, cols, norm_ref, False, p_ref, emit)


def own_kernel(n, first_col, q_all, neg_ref, cols_ref, norm_ref, out_ref, p_ref):
    rows = q_all.shape[0] // n
    runs = runs_of([neg_ref], rows)
    cols = [cols_ref[:, first_col + j : first_col + j + 1] for j in range(len(runs))]

    def emit(j, g):
        out_ref[j * rows : (j + 1) * rows, :] = g

    gradient(n, q_all, runs, cols, norm_ref, False, p_ref, emit)


def items_kernel(n, *refs):
    (q_all, it_o, it_p, cols_ref, norm_ref, ct_ref, p_own, p_par), refs = refs[:8], refs[8:]
    (_, loss_ref, mine_ref, theirs_ref, own_ref), refs = refs[:5], refs[5:]
    msg_refs, (p_ref,) = refs[: n - 1], refs[n - 1 :]
    rows = q_all.shape[0] // n
    negs = p_own.shape[0]

    def emit(j, g):
        if j == 0:
            mine_ref[...] = g
        else:
            theirs_ref[...] = g.astype(BF16)

    cols = [cols_ref[:, j : j + 1] for j in range(2)]
    matched = gradient(n, q_all, runs_of([it_o, it_p], rows), cols, norm_ref, True, p_ref, emit)
    loss_ref[...] = norm_ref[0:1, :] - matched
    for k in range(n):
        part = slice(k * rows, (k + 1) * rows)
        u = jnp.dot(ct_ref[:, : 2 * rows], p_ref[:, part], preferred_element_type=F32)
        u += jnp.dot(ct_ref[:, 2 * rows : 2 * rows + negs], p_own[:, part], preferred_element_type=F32)
        u += jnp.dot(ct_ref[:, 2 * rows + negs :], p_par[:, part], preferred_element_type=F32)
        if k == 0:
            own_ref[...] = u
        else:
            msg_refs[k - 1][...] = u.astype(BF16)


def query_kernel(own_ref, *refs):
    total = own_ref[...]
    for ref in refs[:-1]:
        total = total + ref[...].astype(F32)
    refs[-1][...] = total.T


def local_fn(mesh):
    n_dev, n_grp = mesh.shape["dev"], mesh.shape["grp"]
    n = n_dev // 2
    masks = [1 << i for i in range((n_grp - 1).bit_length())]

    def call(kernel, outs, args, scratch=(), cost=None, smem=0, raw=0):
        shapes = [
            jax.ShapeDtypeStruct(o.shape, o.dtype) if isinstance(o, jax.ShapeDtypeStruct) else pltpu.VMEM(*o)
            for o in outs
        ]
        spec = pl.BlockSpec(memory_space=pltpu.VMEM)
        specs = [pl.BlockSpec(memory_space=pltpu.SMEM)] * smem + [spec] * (len(args) - smem)
        args = list(args[:raw]) + [pltpu.with_memory_space_constraint(a, pltpu.VMEM) for a in args[raw:]]
        flops, exps = cost
        return pl.pallas_call(
            kernel,
            out_shape=shapes,
            in_specs=specs,
            out_specs=[spec] * len(outs),
            scratch_shapes=list(scratch),
            cost_estimate=pl.CostEstimate(flops=flops, bytes_accessed=0, transcendentals=exps),
            compiler_params=pltpu.CompilerParams(vmem_limit_bytes=GRANT),
        )(*args)

    def butterfly(x, t):
        steps = len(masks)
        pairs = []
        for g in range(n_grp):
            for d in range(n_dev):
                mask = masks[(t + d % 2) % steps]
                pairs.append((g * n_dev + d, (g ^ mask) * n_dev + d))
        return lax.ppermute(x, ("grp", "dev"), pairs)

    def local(queries, items, item_ids, neg_embed, neg_logq, logq_table):
        return step(queries, items, item_ids, neg_embed, neg_logq, logq_table)

    def exchange(x, k):
        return swap(x, "dev", n_dev, 2 * k)

    def partner(x):
        return swap(x, "dev", n_dev, 1)

    def step(queries, items, item_ids, neg_embed, neg_logq, logq_table):
        rows, width = queries.shape
        negs = neg_embed.shape[0]
        others = [exchange(queries, k) for k in range(1, n)]
        items_p = partner(items)
        neg_p = partner(neg_embed)
        logq_p = partner(neg_logq)
        lq_o = neg_logq.reshape(negs // rows, rows)
        lq_p = logq_p.reshape(negs // rows, rows)
        table = logq_table.reshape(-1, LANES)
        cands = 2 * (rows + negs)
        unit = 2 * rows * width
        shape = jax.ShapeDtypeStruct

        lse0, cols, c_t, q0, items, neg_embed = call(
            own_block_kernel,
            [
                ((1, rows), F32),
                ((rows, LANES), F32),
                ((width, cands), BF16),
                ((rows, width), BF16),
                ((rows, width), BF16),
                ((negs, width), BF16),
            ],
            (item_ids, table, queries, items, neg_embed, lq_o, items_p, neg_p, lq_p),
            [pltpu.VMEM((2 * rows, LANES), F32), pltpu.VMEM((cands, rows), F32)],
            (unit * cands, rows * cands),
            smem=1,
            raw=6,
        )
        q = [q0] + others
        msg_rows = round_up(3 * n, 16)
        lse, msg = call(
            lambda *r: other_blocks_kernel(n, *r),
            [((n, rows), F32), ((msg_rows, rows), BF16)],
            (*others, items, items_p, neg_embed, neg_p, cols, lse0),
            [pltpu.VMEM((cands, rows), F32)],
            ((n - 1) * unit * cands, (n - 1) * rows * cands),
        )
        got = [exchange(msg, k) for k in range(1, n)]
        per_run = negs // rows
        theirs, p_par, norm, q_all = call(
            lambda *r: partner_kernel(n, 2 + per_run, *r),
            [((negs, width), BF16), ((negs, n * rows), BF16), ((n, rows), F32), ((n * rows, width), BF16)],
            (*q, neg_p, cols, lse, *got),
            (),
            (2 * n * unit * negs, n * rows * negs),
        )
        back = partner(theirs)
        mine, p_own = call(
            lambda *r: own_kernel(n, 2, *r),
            [((negs, width), F32), ((negs, n * rows), BF16)],
            (q_all, neg_embed, cols, norm),
            (),
            (2 * n * unit * negs, n * rows * negs),
        )
        part = (mine + back.astype(F32)).astype(BF16)
        loss, item_mine, item_theirs, u_own, *u_msgs = call(
            lambda *r: items_kernel(n, *r),
            [((1, rows), F32), ((rows, width), F32), ((rows, width), BF16), ((width, rows), F32)]
            + [((width, rows), BF16)] * (n - 1),
            (q_all, items, items_p, cols, norm, c_t, p_own, p_par, part),
            [pltpu.VMEM((2 * rows, n * rows), BF16)],
            (3 * n * unit * cands, 2 * n * rows * rows),
        )
        item_back = partner(item_theirs)
        u_got = [exchange(u_msgs[k - 1], k) for k in range(1, n)]
        (query_grad,) = call(query_kernel, [shape((rows, width), F32)], (u_own, *u_got), (), (n * rows * width, 0))
        for t in range(len(masks)):
            other = butterfly(part, t)
            total = part.astype(F32) + other.astype(F32)
            part = total.astype(BF16)
        item_grad = item_mine + item_back.astype(F32)
        return (loss.reshape(rows), query_grad, item_grad, total)

    return local


def solution(mesh):
    return jax.shard_map(
        local_fn(mesh),
        mesh=mesh,
        in_specs=(
            P(("grp", "dev"), None),
            P(("grp", "dev"), None),
            P("grp"),
            P("dev", None),
            P("dev"),
            P(),
        ),
        out_specs=(
            P(("grp", "dev")),
            P(("grp", "dev"), None),
            P(("grp", "dev"), None),
            P("dev", None),
        ),
        check_vma=False,
    )
```

```python
import jax
import jax.numpy as jnp
from jax import lax
from jax.experimental import pallas as pl
from jax.experimental.pallas import tpu as pltpu
from jax.sharding import PartitionSpec as P

logit_scale = 0.25
LANES = 128
F32, BF16 = jnp.float32, jnp.bfloat16
NT = (((1,), (1,)), ((), ()))
GRANT = 16 << 20


def round_up(x, m):
    return -(-x // m) * m


def swap(x, axis, count, mask):
    return lax.ppermute(x, axis, [(i, i ^ mask) for i in range(count)])


def fold(x, op):
    rows, cols = x.shape
    return op(x.reshape(rows // 8, 8, cols), axis=0)


def pad_rows(parts, multiple):
    have = sum(p.shape[0] for p in parts)
    lack = round_up(have, multiple) - have
    if lack:
        parts = parts + [jnp.zeros((lack, parts[0].shape[1]), parts[0].dtype)]
    return jnp.concatenate(parts, axis=0)


def split3(x):
    hi = x.astype(BF16)
    rest = x - hi.astype(F32)
    mid = rest.astype(BF16)
    return [hi, mid, (rest - mid.astype(F32)).astype(BF16)]


def runs_of(refs, rows):
    return [(ref, first) for ref in refs for first in range(0, ref.shape[0], rows)]


def prepare_kernel(ids_ref, table_hbm, q_hbm, it_hbm, neg_hbm, lq_hbm, *refs):
    q_ref, it_ref, neg_ref, cols_ref, table, lq, picked, sems = refs
    copies = [
        pltpu.make_async_copy(src, dst, sems.at[i])
        for i, (src, dst) in enumerate(
            [(table_hbm, table), (lq_hbm, lq), (q_hbm, q_ref), (it_hbm, it_ref), (neg_hbm, neg_ref)]
        )
    ]
    for c in copies:
        c.start()
    copies[0].wait()
    copies[1].wait()
    rows, _ = q_ref.shape
    dev = lax.axis_index("dev")
    lane = lax.broadcasted_iota(jnp.int32, (1, LANES), 1)
    for half, owner in enumerate((dev, dev ^ 1)):
        start = owner * rows

        def pick(i, carry, half=half, start=start):
            for t in range(8):
                j = i * 8 + t
                item = ids_ref[start + j]
                row = table[pl.ds(lax.shift_right_logical(item, 7), 1), :]
                picked[pl.ds(half * rows + j, 1), :] = jnp.where(lane == (item & (LANES - 1)), row, 0.0)
            return carry

        lax.fori_loop(0, rows // 8, pick, 0)
    for half in range(2):
        part = picked[half * rows : (half + 1) * rows, :]
        cols_ref[:, half : half + 1] = jnp.sum(part, axis=1, keepdims=True)
    own = lq.shape[0]
    cols_ref[:, 2 : 2 + own] = pad_rows([lq[...]], 8).T[:, :own]
    for c in copies[2:]:
        c.wait()


def first_pass(runs, cols, q, e_ref, diagonal):
    rows = q.shape[0]
    top, matched = None, None
    for j, (ref, first) in enumerate(runs):
        s = lax.dot_general(ref[first : first + rows, :], q, NT, preferred_element_type=F32)
        s = logit_scale * s - cols[j]
        e_ref[j * rows : (j + 1) * rows, :] = s
        here = fold(s, jnp.max)
        top = here if top is None else jnp.maximum(top, here)
        if diagonal and j == 0:
            matched = jnp.sum(jnp.where(own_mask(rows), s, 0.0), axis=0, keepdims=True)
    row_max = jnp.max(top, axis=0, keepdims=True)
    total = None
    for j in range(len(runs)):
        e = jnp.exp(e_ref[j * rows : (j + 1) * rows, :] - row_max)
        e_ref[j * rows : (j + 1) * rows, :] = e
        here = fold(e, jnp.sum)
        total = here if total is None else total + here
    return row_max, row_max + jnp.log(jnp.sum(total, axis=0, keepdims=True)), matched


def own_mask(rows):
    shape = (rows, rows)
    return lax.broadcasted_iota(jnp.int32, shape, 0) == lax.broadcasted_iota(jnp.int32, shape, 1)


def candidate_cols(own_ref, partner_ref, negs):
    return (
        [own_ref[:, j : j + 1] for j in range(2 + negs)]
        + [partner_ref[:, j : j + 1] for j in range(negs)]
    )


def own_block_kernel(q_ref, it_o, it_p, neg_o, neg_p, cols_own, lq_p, *refs):
    stat_ref, e_ref, ct_ref, cols_ref = refs
    rows, _ = q_ref.shape
    negs = lq_p.shape[0]
    cols_ref[:, :negs] = pad_rows([lq_p[...]], 8).T[:, :negs]
    runs = runs_of((it_o, it_p, neg_o, neg_p), rows)
    cols = candidate_cols(cols_own, cols_ref, negs)
    stat_ref[0:1, :], stat_ref[1:2, :], stat_ref[2:3, :] = first_pass(runs, cols, q_ref[...], e_ref, True)
    for j, (ref, first) in enumerate(runs):
        ct_ref[:, j * rows : (j + 1) * rows] = ref[first : first + rows, :].T


def other_blocks_kernel(n, *refs):
    q_refs, refs = refs[: n - 1], refs[n - 1 :]
    c_refs, (cols_own, cols_par, stat0_ref), refs = refs[:4], refs[4:7], refs[7:]
    max_ref, lse_ref, msg_ref, e_refs = refs[0], refs[1], refs[2], refs[3:]
    rows, _ = q_refs[0].shape
    runs = runs_of(c_refs, rows)
    cols = candidate_cols(cols_own, cols_par, c_refs[2].shape[0] // rows)
    max_ref[0:1, :] = stat0_ref[0:1, :]
    lse_ref[0:1, :] = stat0_ref[1:2, :]
    for k in range(1, n):
        top, lse, _ = first_pass(runs, cols, q_refs[k - 1][...], e_refs[k - 1], False)
        max_ref[k : k + 1, :] = top
        lse_ref[k : k + 1, :] = lse
    msg_ref[...] = pad_rows(split3(lse_ref[...]), 16)


def second_pass(n, e_refs, offset, q_all, weight_ref, mask_first, p_ref, emit):
    rows = q_all.shape[0] // n
    for j in range(p_ref.shape[0] // rows):
        run = slice(j * rows, (j + 1) * rows)
        src = slice(offset + j * rows, offset + (j + 1) * rows)
        for b in range(n):
            p = e_refs[b][src, :] * weight_ref[b : b + 1, :]
            if mask_first and j == 0 and b == 0:
                p = p - jnp.where(own_mask(rows), logit_scale, 0.0)
            p_ref[run, b * rows : (b + 1) * rows] = p.astype(BF16)
        emit(j, jnp.dot(p_ref[run, :], q_all[...], preferred_element_type=F32))


def partner_kernel(n, offset, *refs):
    q_refs, e_refs, refs = refs[:n], refs[n : 2 * n], refs[2 * n :]
    max_ref, lse_ref, stat0_ref, refs = refs[0], refs[1], refs[2], refs[3:]
    got_refs, (out_ref, p_ref, weight_ref, loss_ref, q_all) = refs[: n - 1], refs[n - 1 :]
    rows, _ = q_refs[0].shape
    for k in range(n):
        q_all[k * rows : (k + 1) * rows, :] = q_refs[k][...]
    totals = [lse_ref[...]]
    for ref in got_refs:
        got = ref[...].astype(F32)
        totals.append(got[:n] + got[n : 2 * n] + got[2 * n : 3 * n])
    for b in range(n):
        parts = [totals[k][k ^ b : (k ^ b) + 1, :] for k in range(n)]
        top = parts[0]
        for r in parts[1:]:
            top = jnp.maximum(top, r)
        total = jnp.exp(parts[0] - top)
        for r in parts[1:]:
            total = total + jnp.exp(r - top)
        norm = top + jnp.log(total)
        weight_ref[b : b + 1, :] = logit_scale * jnp.exp(max_ref[b : b + 1, :] - norm)
        if b == 0:
            loss_ref[...] = norm - stat0_ref[2:3, :]

    def emit(j, g):
        out_ref[j * rows : (j + 1) * rows, :] = g.astype(BF16)

    second_pass(n, e_refs, offset, q_all, weight_ref, False, p_ref, emit)


def own_kernel(n, offset, q_all, weight_ref, *refs):
    e_refs, (out_ref, p_ref) = refs[:n], refs[n:]
    rows = q_all.shape[0] // n

    def emit(j, g):
        out_ref[j * rows : (j + 1) * rows, :] = g

    second_pass(n, e_refs, offset, q_all, weight_ref, False, p_ref, emit)


def items_kernel(n, q_all, weight_ref, ct_ref, p_own, p_par, _, *refs):
    e_refs, refs = refs[:n], refs[n:]
    (mine_ref, theirs_ref, own_ref), refs = refs[:3], refs[3:]
    msg_refs, (p_ref,) = refs[: n - 1], refs[n - 1 :]
    rows = q_all.shape[0] // n
    negs = p_own.shape[0]

    def emit(j, g):
        if j == 0:
            mine_ref[...] = g
        else:
            theirs_ref[...] = g.astype(BF16)

    second_pass(n, e_refs, 0, q_all, weight_ref, True, p_ref, emit)
    for k in range(n):
        part = slice(k * rows, (k + 1) * rows)
        u = jnp.dot(ct_ref[:, : 2 * rows], p_ref[:, part], preferred_element_type=F32)
        u += jnp.dot(ct_ref[:, 2 * rows : 2 * rows + negs], p_own[:, part], preferred_element_type=F32)
        u += jnp.dot(ct_ref[:, 2 * rows + negs :], p_par[:, part], preferred_element_type=F32)
        if k == 0:
            own_ref[...] = u
        else:
            msg_refs[k - 1][...] = u.astype(BF16)


def outputs_kernel(loss_in, mine_ref, back_ref, own_ref, *refs):
    loss_ref, query_ref, item_ref = refs[-3:]
    loss_ref[...] = loss_in[...]
    item_ref[...] = mine_ref[...] + back_ref[...].astype(F32)
    total = own_ref[...]
    for ref in refs[:-3]:
        total = total + ref[...].astype(F32)
    query_ref[...] = total.T


def local_fn(mesh):
    n_dev, n_grp = mesh.shape["dev"], mesh.shape["grp"]
    n = n_dev // 2
    masks = [1 << i for i in range((n_grp - 1).bit_length())]

    def call(kernel, outs, args, scratch, cost, specs=None):
        shapes = [o if isinstance(o, jax.ShapeDtypeStruct) else pltpu.VMEM(*o) for o in outs]
        vmem = pl.BlockSpec(memory_space=pltpu.VMEM)
        place = pltpu.VMEM if specs is None else pltpu.HBM
        flops, exps = cost
        return pl.pallas_call(
            kernel,
            out_shape=shapes,
            in_specs=specs or [vmem] * len(args),
            out_specs=[vmem] * len(outs),
            scratch_shapes=list(scratch),
            cost_estimate=pl.CostEstimate(flops=flops, bytes_accessed=0, transcendentals=exps),
            compiler_params=pltpu.CompilerParams(vmem_limit_bytes=GRANT),
        )(*[pltpu.with_memory_space_constraint(a, place) for a in args])

    def butterfly(x, t):
        steps = len(masks)
        pairs = []
        for g in range(n_grp):
            for d in range(n_dev):
                mask = masks[(t + d % 2) % steps]
                pairs.append((g * n_dev + d, (g ^ mask) * n_dev + d))
        return lax.ppermute(x, ("grp", "dev"), pairs)

    def local(queries, items, item_ids, neg_embed, neg_logq, logq_table):
        return step(queries, items, item_ids, neg_embed, neg_logq, logq_table)

    def exchange(x, k):
        return swap(x, "dev", n_dev, 2 * k)

    def partner(x):
        return swap(x, "dev", n_dev, 1)

    def step(queries, items, item_ids, neg_embed, neg_logq, logq_table):
        rows, width = queries.shape
        negs = neg_embed.shape[0]
        others = [exchange(queries, k) for k in range(1, n)]
        items_p = partner(items)
        neg_p = partner(neg_embed)
        logq_p = partner(neg_logq)
        cands = 2 * (rows + negs)
        unit = 2 * rows * width
        per_run = negs // rows
        shape = jax.ShapeDtypeStruct
        hbm = pl.BlockSpec(memory_space=pl.ANY)
        table_shape = (logq_table.size // LANES, LANES)

        q0, items, neg_embed, cols = call(
            prepare_kernel,
            [((rows, width), BF16), ((rows, width), BF16), ((negs, width), BF16), ((rows, LANES), F32)],
            (
                item_ids,
                logq_table.reshape(table_shape),
                queries,
                items,
                neg_embed,
                neg_logq.reshape(per_run, rows),
            ),
            [
                pltpu.VMEM(table_shape, F32),
                pltpu.VMEM((per_run, rows), F32),
                pltpu.VMEM((2 * rows, LANES), F32),
                pltpu.SemaphoreType.DMA((5,)),
            ],
            (rows * LANES, 0),
            [pl.BlockSpec(memory_space=pltpu.SMEM)] + [hbm] * 5,
        )
        cand_refs = (items, items_p, neg_embed, neg_p)
        stat0, e0, c_t, cols_p = call(
            own_block_kernel,
            [((3, rows), F32), ((cands, rows), F32), ((width, cands), BF16), ((rows, LANES), F32)],
            (q0, *cand_refs, cols, logq_p.reshape(per_run, rows)),
            (),
            (unit * cands, rows * cands),
        )
        msg_rows = round_up(3 * n, 16)
        tops, lse, msg, *e_rest = call(
            lambda *r: other_blocks_kernel(n, *r),
            [((n, rows), F32), ((n, rows), F32), ((msg_rows, rows), BF16)]
            + [((cands, rows), F32)] * (n - 1),
            (*others, *cand_refs, cols, cols_p, stat0),
            (),
            ((n - 1) * unit * cands, (n - 1) * rows * cands),
        )
        e = (e0, *e_rest)
        got = [exchange(msg, k) for k in range(1, n)]
        theirs, p_par, weight, loss, q_all = call(
            lambda *r: partner_kernel(n, 2 * rows + negs, *r),
            [
                ((negs, width), BF16),
                ((negs, n * rows), BF16),
                ((n, rows), F32),
                ((1, rows), F32),
                ((n * rows, width), BF16),
            ],
            (q0, *others, *e, tops, lse, stat0, *got),
            (),
            (n * unit * negs, 0),
        )
        back = partner(theirs)
        mine, p_own = call(
            lambda *r: own_kernel(n, 2 * rows, *r),
            [((negs, width), F32), ((negs, n * rows), BF16)],
            (q_all, weight, *e),
            (),
            (n * unit * negs, 0),
        )
        part = (mine + back.astype(F32)).astype(BF16)
        item_mine, item_theirs, u_own, *u_msgs = call(
            lambda *r: items_kernel(n, *r),
            [((rows, width), F32), ((rows, width), BF16), ((width, rows), F32)]
            + [((width, rows), BF16)] * (n - 1),
            (q_all, weight, c_t, p_own, p_par, part, *e),
            [pltpu.VMEM((2 * rows, n * rows), BF16)],
            (2 * n * unit * cands, 0),
        )
        item_back = partner(item_theirs)
        u_got = [exchange(u_msgs[k - 1], k) for k in range(1, n)]
        loss, query_grad, item_grad = call(
            outputs_kernel,
            [shape((1, rows), F32), shape((rows, width), F32), shape((rows, width), F32)],
            (loss, item_mine, item_back, u_own, *u_got),
            (),
            (n * rows * width, 0),
        )
        for t in range(len(masks)):
            other = butterfly(part, t)
            total = part.astype(F32) + other.astype(F32)
            part = total.astype(BF16)
        return (loss.reshape(rows), query_grad, item_grad, total)

    return local


def solution(mesh):
    return jax.shard_map(
        local_fn(mesh),
        mesh=mesh,
        in_specs=(
            P(("grp", "dev"), None),
            P(("grp", "dev"), None),
            P("grp"),
            P("dev", None),
            P("dev"),
            P(),
        ),
        out_specs=(
            P(("grp", "dev")),
            P(("grp", "dev"), None),
            P(("grp", "dev"), None),
            P("dev", None),
        ),
        check_vma=False,
    )
```

```python
import jax
import jax.numpy as jnp
from jax import lax
from jax.experimental import pallas as pl
from jax.experimental.pallas import tpu as pltpu
from jax.sharding import PartitionSpec as P

logit_scale = 0.25
LANES = 128
F32, BF16 = jnp.float32, jnp.bfloat16
NT = (((1,), (1,)), ((), ()))
GRANT = 16 << 20


def round_up(x, m):
    return -(-x // m) * m


def swap(x, axis, count, mask):
    return lax.ppermute(x, axis, [(i, i ^ mask) for i in range(count)])


def fold(x, op):
    rows, cols = x.shape
    return op(x.reshape(rows // 8, 8, cols), axis=0)


def pad_rows(parts, multiple):
    have = sum(p.shape[0] for p in parts)
    lack = round_up(have, multiple) - have
    if lack:
        parts = parts + [jnp.zeros((lack, parts[0].shape[1]), parts[0].dtype)]
    return jnp.concatenate(parts, axis=0)


def split3(x):
    hi = x.astype(BF16)
    rest = x - hi.astype(F32)
    mid = rest.astype(BF16)
    return [hi, mid, (rest - mid.astype(F32)).astype(BF16)]


def runs_of(refs, rows):
    return [(ref, first) for ref in refs for first in range(0, ref.shape[0], rows)]


def prepare_kernel(chunks, ids_hbm, table_hbm, q_hbm, it_hbm, neg_hbm, lq_hbm, *refs):
    q_ref, it_ref, neg_ref, cols_ref, ids, table, lq, picked, sems = refs
    part = table.shape[0] // chunks
    moves = [(ids_hbm, ids), (lq_hbm, lq)]
    moves += [
        (table_hbm.at[pl.ds(i * part, part), :], table.at[pl.ds(i * part, part), :]) for i in range(chunks)
    ]
    moves += [(q_hbm, q_ref), (it_hbm, it_ref), (neg_hbm, neg_ref)]
    copies = [pltpu.make_async_copy(src, dst, sems.at[i]) for i, (src, dst) in enumerate(moves)]
    for c in copies:
        c.start()
    for c in copies[: 2 + chunks]:
        c.wait()
    rows, _ = q_ref.shape
    dev = lax.axis_index("dev")
    lane = lax.broadcasted_iota(jnp.int32, (1, LANES), 1)
    for half, owner in enumerate((dev, dev ^ 1)):
        start = owner * rows
        for j in range(rows):
            item = ids[start + j]
            row = table[pl.ds(lax.shift_right_logical(item, 7), 1), :]
            at = half * rows + j
            picked[at : at + 1, :] = jnp.where(lane == (item & (LANES - 1)), row, 0.0)
    for half in range(2):
        run = picked[half * rows : (half + 1) * rows, :]
        cols_ref[:, half : half + 1] = jnp.sum(run, axis=1, keepdims=True)
    own = lq.shape[0]
    cols_ref[:, 2 : 2 + own] = pad_rows([lq[...]], 8).T[:, :own]
    for c in copies[2 + chunks :]:
        c.wait()


def first_pass(runs, cols, q, e_ref, diagonal):
    rows = q.shape[0]
    top, matched = None, None
    for j, (ref, first) in enumerate(runs):
        s = lax.dot_general(ref[first : first + rows, :], q, NT, preferred_element_type=F32)
        s = logit_scale * s - cols[j]
        e_ref[j * rows : (j + 1) * rows, :] = s
        here = fold(s, jnp.max)
        top = here if top is None else jnp.maximum(top, here)
        if diagonal and j == 0:
            matched = jnp.sum(jnp.where(own_mask(rows), s, 0.0), axis=0, keepdims=True)
    row_max = jnp.max(top, axis=0, keepdims=True)
    total = None
    for j in range(len(runs)):
        e = jnp.exp(e_ref[j * rows : (j + 1) * rows, :] - row_max)
        e_ref[j * rows : (j + 1) * rows, :] = e
        here = fold(e, jnp.sum)
        total = here if total is None else total + here
    row_sum = jnp.sum(total, axis=0, keepdims=True)
    return row_max, row_max + jnp.log(row_sum), matched, row_sum


def own_mask(rows):
    shape = (rows, rows)
    return lax.broadcasted_iota(jnp.int32, shape, 0) == lax.broadcasted_iota(jnp.int32, shape, 1)


def candidate_cols(own_ref, partner_ref, negs):
    return (
        [own_ref[:, j : j + 1] for j in range(2 + negs)]
        + [partner_ref[:, j : j + 1] for j in range(negs)]
    )


def own_block_kernel(q_ref, it_o, it_p, neg_o, neg_p, cols_own, lq_p, *refs):
    stat_ref, e_ref, ct_ref, cols_ref = refs
    rows, _ = q_ref.shape
    negs = lq_p.shape[0]
    cols_ref[:, :negs] = pad_rows([lq_p[...]], 8).T[:, :negs]
    runs = runs_of((it_o, it_p, neg_o, neg_p), rows)
    cols = candidate_cols(cols_own, cols_ref, negs)
    top, lse, matched, _ = first_pass(runs, cols, q_ref[...], e_ref, True)
    stat_ref[0:1, :] = top
    stat_ref[1:2, :] = lse
    stat_ref[2:3, :] = matched
    for j, (ref, first) in enumerate(runs):
        ct_ref[:, j * rows : (j + 1) * rows] = ref[first : first + rows, :].T


def other_blocks_kernel(count, near, *refs):
    q_refs, refs = refs[:count], refs[count:]
    c_refs, (cols_own, cols_par), refs = refs[:4], refs[4:6], refs[6:]
    rows, _ = q_refs[0].shape
    runs = runs_of(c_refs, rows)
    cols = candidate_cols(cols_own, cols_par, c_refs[2].shape[0] // rows)
    if near is not None:
        ct_ref, refs = refs[0], refs[1:]
    stat_ref, e_refs, rest = refs[0], refs[1 : 1 + count], refs[1 + count :]
    for i in range(count):
        top, lse, _, total = first_pass(runs, cols, q_refs[i][...], e_refs[i], False)
        stat_ref[2 * i : 2 * i + 1, :] = top
        stat_ref[2 * i + 1 : 2 * i + 2, :] = lse
        if i == near:
            u = jnp.dot(ct_ref[...], e_refs[i][...].astype(BF16), preferred_element_type=F32)
            rest[0][...] = (u * (1.0 / total)).astype(BF16)


def last_block_kernel(n, order, q_ref, *refs):
    c_refs, (cols_own, cols_par, stat0, stat_rest, near_u), refs = refs[:4], refs[4:9], refs[9:]
    max_ref, lse_ref, msg_ref, near_ref, e_ref = refs
    rows, _ = q_ref.shape
    runs = runs_of(c_refs, rows)
    cols = candidate_cols(cols_own, cols_par, c_refs[2].shape[0] // rows)
    last = first_pass(runs, cols, q_ref[...], e_ref, False)
    for k in range(n):
        if k == 0:
            top, lse = stat0[0:1, :], stat0[1:2, :]
        elif k == order[-1]:
            top, lse = last[:2]
        else:
            i = order.index(k)
            top, lse = stat_rest[2 * i : 2 * i + 1, :], stat_rest[2 * i + 1 : 2 * i + 2, :]
        max_ref[k : k + 1, :] = top
        lse_ref[k : k + 1, :] = lse
    width = near_u.shape[0]
    near_ref[:width, :] = near_u[...]
    msg = pad_rows(split3(lse_ref[...]), 16)
    msg_ref[...] = msg
    near_ref[width:, :] = msg


def second_pass(n, e_refs, offset, q_all, weight_ref, mask_first, p_ref, emit):
    rows = q_all.shape[0] // n
    for j in range(p_ref.shape[0] // rows):
        run = slice(j * rows, (j + 1) * rows)
        src = slice(offset + j * rows, offset + (j + 1) * rows)
        for b in range(n):
            p = e_refs[b][src, :] * weight_ref[b : b + 1, :]
            if mask_first and j == 0 and b == 0:
                p = p - jnp.where(own_mask(rows), logit_scale, 0.0)
            p_ref[run, b * rows : (b + 1) * rows] = p.astype(BF16)
        emit(j, jnp.dot(p_ref[run, :], q_all[...], preferred_element_type=F32))


def partner_kernel(n, offset, width, *refs):
    q_refs, e_refs, refs = refs[:n], refs[n : 2 * n], refs[2 * n :]
    max_ref, lse_ref, stat0_ref, refs = refs[0], refs[1], refs[2], refs[3:]
    got_refs, (out_ref, p_ref, weight_ref, loss_ref, near_ref, q_all) = refs[: n - 1], refs[n - 1 :]
    rows, _ = q_refs[0].shape
    for k in range(n):
        q_all[k * rows : (k + 1) * rows, :] = q_refs[k][...]
    totals = [lse_ref[...]]
    for k, ref in enumerate(got_refs):
        got = (ref[width:, :] if k == 0 else ref[...]).astype(F32)
        totals.append(got[:n] + got[n : 2 * n] + got[2 * n : 3 * n])
    for b in range(n):
        parts = [totals[k][k ^ b : (k ^ b) + 1, :] for k in range(n)]
        top = parts[0]
        for r in parts[1:]:
            top = jnp.maximum(top, r)
        total = jnp.exp(parts[0] - top)
        for r in parts[1:]:
            total = total + jnp.exp(r - top)
        norm = top + jnp.log(total)
        weight_ref[b : b + 1, :] = logit_scale * jnp.exp(max_ref[b : b + 1, :] - norm)
        if b == 0:
            loss_ref[...] = norm - stat0_ref[2:3, :]
            near_ref[...] = logit_scale * jnp.exp(totals[1][1:2, :] - norm)

    def emit(j, g):
        out_ref[j * rows : (j + 1) * rows, :] = g.astype(BF16)

    second_pass(n, e_refs, offset, q_all, weight_ref, False, p_ref, emit)


def own_kernel(n, q_all, weight_ref, *refs):
    e_refs, (out_ref, p_ref, mine_ref, theirs_ref, p_items) = refs[:n], refs[n:]
    rows = q_all.shape[0] // n

    def emit(j, g):
        out_ref[j * rows : (j + 1) * rows, :] = g

    def emit_item(j, g):
        if j == 0:
            mine_ref[...] = g
        else:
            theirs_ref[...] = g.astype(BF16)

    second_pass(n, e_refs, 2 * rows, q_all, weight_ref, False, p_ref, emit)
    second_pass(n, e_refs, 0, q_all, weight_ref, True, p_items, emit_item)


def partial_kernel(blocks, ct_ref, p_items, p_own, p_par, *out_refs):
    rows = out_refs[0].shape[1]
    item_rows, negs = p_items.shape[0], p_own.shape[0]
    for k, out_ref in zip(blocks, out_refs):
        part = slice(k * rows, (k + 1) * rows)
        u = jnp.dot(ct_ref[:, :item_rows], p_items[:, part], preferred_element_type=F32)
        u += jnp.dot(ct_ref[:, item_rows : item_rows + negs], p_own[:, part], preferred_element_type=F32)
        u += jnp.dot(ct_ref[:, item_rows + negs :], p_par[:, part], preferred_element_type=F32)
        out_ref[...] = u.astype(out_ref.dtype)


def outputs_kernel(loss_in, mine_ref, back_ref, own_ref, near_w, near_u, *refs):
    loss_ref, query_ref, item_ref = refs[-3:]
    loss_ref[...] = loss_in[...]
    item_ref[...] = mine_ref[...] + back_ref[...].astype(F32)
    width = own_ref.shape[0]
    total = own_ref[...] + near_w[...] * near_u[:width, :].astype(F32)
    for ref in refs[:-3]:
        total = total + ref[...].astype(F32)
    query_ref[...] = total.T


def local_fn(mesh):
    n_dev, n_grp = mesh.shape["dev"], mesh.shape["grp"]
    n = n_dev // 2
    masks = [1 << i for i in range((n_grp - 1).bit_length())]

    def call(kernel, outs, args, scratch, cost, specs=None):
        shapes = [o if isinstance(o, jax.ShapeDtypeStruct) else pltpu.VMEM(*o) for o in outs]
        vmem = pl.BlockSpec(memory_space=pltpu.VMEM)
        place = pltpu.VMEM if specs is None else pltpu.HBM
        flops, exps = cost
        return pl.pallas_call(
            kernel,
            out_shape=shapes,
            in_specs=specs or [vmem] * len(args),
            out_specs=[vmem] * len(outs),
            scratch_shapes=list(scratch),
            cost_estimate=pl.CostEstimate(flops=flops, bytes_accessed=0, transcendentals=exps),
            compiler_params=pltpu.CompilerParams(vmem_limit_bytes=GRANT),
        )(*[pltpu.with_memory_space_constraint(a, place) for a in args])

    def butterfly(x, t):
        steps = len(masks)
        pairs = []
        for g in range(n_grp):
            for d in range(n_dev):
                mask = masks[(t + d % 2) % steps]
                pairs.append((g * n_dev + d, (g ^ mask) * n_dev + d))
        return lax.ppermute(x, ("grp", "dev"), pairs)

    def local(queries, items, item_ids, neg_embed, neg_logq, logq_table):
        return step(queries, items, item_ids, neg_embed, neg_logq, logq_table)

    def exchange(x, k):
        return swap(x, "dev", n_dev, 2 * k)

    def partner(x):
        return swap(x, "dev", n_dev, 1)

    def step(queries, items, item_ids, neg_embed, neg_logq, logq_table):
        rows, width = queries.shape
        negs = neg_embed.shape[0]
        others = [exchange(queries, k) for k in range(1, n)]
        items_p = partner(items)
        neg_p = partner(neg_embed)
        logq_p = partner(neg_logq)
        cands = 2 * (rows + negs)
        unit = 2 * rows * width
        per_run = negs // rows
        shape = jax.ShapeDtypeStruct
        hbm = pl.BlockSpec(memory_space=pl.ANY)
        table_shape = (logq_table.size // LANES, LANES)

        chunks = 4 if table_shape[0] % 32 == 0 else 1

        q0, items, neg_embed, cols = call(
            lambda *r: prepare_kernel(chunks, *r),
            [((rows, width), BF16), ((rows, width), BF16), ((negs, width), BF16), ((rows, LANES), F32)],
            (
                item_ids,
                logq_table.reshape(table_shape),
                queries,
                items,
                neg_embed,
                neg_logq.reshape(per_run, rows),
            ),
            [
                pltpu.SMEM(item_ids.shape, jnp.int32),
                pltpu.VMEM(table_shape, F32),
                pltpu.VMEM((per_run, rows), F32),
                pltpu.VMEM((2 * rows, LANES), F32),
                pltpu.SemaphoreType.DMA((5 + chunks,)),
            ],
            (rows * LANES, 0),
            [hbm] * 6,
        )
        cand_refs = (items, items_p, neg_embed, neg_p)
        stat0, e0, c_t, cols_p = call(
            own_block_kernel,
            [((3, rows), F32), ((cands, rows), F32), ((width, cands), BF16), ((rows, LANES), F32)],
            (q0, *cand_refs, cols, logq_p.reshape(per_run, rows)),
            (),
            (unit * cands, rows * cands),
        )
        last = n // 2
        order = [k for k in range(1, n) if k != last] + [last]
        many = n - 2
        stat_rest, *rest = call(
            lambda *r: other_blocks_kernel(many, 0, *r),
            [((2 * many, rows), F32)] + [((cands, rows), F32)] * many + [((width, rows), BF16)],
            (*[others[k - 1] for k in order[:-1]], *cand_refs, cols, cols_p, c_t),
            (),
            (many * unit * cands, many * rows * cands),
        )
        msg_rows = round_up(3 * n, 16)
        tops, lse, msg, near_msg, e_last = call(
            lambda *r: last_block_kernel(n, order, *r),
            [
                ((n, rows), F32),
                ((n, rows), F32),
                ((msg_rows, rows), BF16),
                ((width + msg_rows, rows), BF16),
                ((cands, rows), F32),
            ],
            (others[last - 1], *cand_refs, cols, cols_p, stat0, stat_rest, rest[-1]),
            (),
            (unit * cands, rows * cands),
        )
        by_block = dict(zip(order, [*rest[:-1], e_last]))
        e = (e0, *[by_block[k] for k in range(1, n)])
        got = [exchange(near_msg if k == 1 else msg, k) for k in range(1, n)]
        theirs, p_par, weight, loss, near_w, q_all = call(
            lambda *r: partner_kernel(n, 2 * rows + negs, width, *r),
            [
                ((negs, width), BF16),
                ((negs, n * rows), BF16),
                ((n, rows), F32),
                ((1, rows), F32),
                ((1, rows), F32),
                ((n * rows, width), BF16),
            ],
            (q0, *others, *e, tops, lse, stat0, *got),
            (),
            (n * unit * negs, 0),
        )
        back = partner(theirs)
        mine, p_own, item_mine, item_theirs, p_items = call(
            lambda *r: own_kernel(n, *r),
            [
                ((negs, width), F32),
                ((negs, n * rows), BF16),
                ((rows, width), F32),
                ((rows, width), BF16),
                ((2 * rows, n * rows), BF16),
            ],
            (q_all, weight, *e),
            (),
            (n * unit * (negs + 2 * rows), 0),
        )
        blocks = [0] + list(range(2, n))
        u_own, *u_msgs = call(
            lambda *r: partial_kernel(blocks, *r),
            [((width, rows), F32)] + [((width, rows), BF16)] * (n - 2),
            (c_t, p_items, p_own, p_par),
            (),
            ((n - 1) * unit * cands, 0),
        )
        part = (mine + back.astype(F32)).astype(BF16)
        item_back = partner(item_theirs)
        u_got = [exchange(u, k) for k, u in zip(blocks[1:], u_msgs)]
        loss, query_grad, item_grad = call(
            outputs_kernel,
            [shape((1, rows), F32), shape((rows, width), F32), shape((rows, width), F32)],
            (loss, item_mine, item_back, u_own, near_w, got[0], *u_got),
            (),
            (n * rows * width, 0),
        )
        for t in range(len(masks)):
            other = butterfly(part, t)
            total = part.astype(F32) + other.astype(F32)
            part = total.astype(BF16)
        return (loss.reshape(rows), query_grad, item_grad, total)

    return local


def solution(mesh):
    return jax.shard_map(
        local_fn(mesh),
        mesh=mesh,
        in_specs=(
            P(("grp", "dev"), None),
            P(("grp", "dev"), None),
            P("grp"),
            P("dev", None),
            P("dev"),
            P(),
        ),
        out_specs=(
            P(("grp", "dev")),
            P(("grp", "dev"), None),
            P(("grp", "dev"), None),
            P("dev", None),
        ),
        check_vma=False,
    )
```
